128 devices in a mesh: pool: 8 (over x, core), wide: 8 (over y, z_hi), narrow: 2 (over z_lo).
Axes of the slice: x: 4, y: 4, z: 4 (z_hi: 2, z_lo: 2; z = z_hi * 2 + z_lo), core: 2. Of those that a mesh axis runs over, the one named last changes fastest.
Arguments:
- states: bfloat16 [384, 2560], P('pool'), may hold values from -3 to 3
- gain_in: float32 [2560], replicated, may hold values from 0.1 to 1.9
- w_qkv: bfloat16 [2560, 8, 6, 128], P('narrow', 'wide'), may hold values from -0.125 to 0.125
- q_gain: float32 [128], replicated, may hold values from 0.1 to 1.9
- k_gain: float32 [128], replicated, may hold values from 0.1 to 1.9
- key_cache: bfloat16 [2304, 8, 128, 128], P('pool', 'wide', 'narrow'), as said below
- value_cache: bfloat16 [2304, 8, 128, 128], P('pool', 'wide', 'narrow'), may hold values from -12 to 12
- cache_len: int32 [384], replicated, may hold values from 1 to 8192, as said below
- page_table: int32 [384, 64], replicated, may hold values from -1 to 2303, as said below
- w_out: bfloat16 [4096, 2560], P('wide'), may hold values from -0.125 to 0.125
- gain_post: float32 [2560], replicated, may hold values from 0.1 to 1.9
- w_gate_up: bfloat16 [2560, 2, 9728], P(None, None, ('wide', 'narrow')), may hold values from -0.125 to 0.125
- w_down: bfloat16 [9728, 2560], P(('wide', 'narrow')), may hold values from -0.078125 to 0.078125
Outputs:
- attn_mixed: bfloat16 [384, 2560], P('pool')
- layer_out: bfloat16 [384, 2560], P('pool')
The draws below stay inside these ranges and needn't reach their ends.
Inputs may be any that keep to these rules, and one draw needn't show every extreme that they name: `cache_len`: exactly one request has 8192 cached tokens; every other request has at most (5) * 128. `page_table`: entry (r, b) is pool device times 288 plus slot of the page with tokens b * 128 to (b + 1) * 128 - 1 of request r for b < ceil(cache_len[r] / 128), and -1 for later b; no slot is named twice. One pool device holds exactly 288 pages; the others hold the remaining pages, within one page of each other. `key_cache`: cached keys.
All inputs are finite; a program needn't handle non-finite values.
Results may differ from the reference program's by a relative error of at most 0.012.
The reference program's roundings to bfloat16 on the way (of `normed`, `query`, `key_new`, `value_new`, `weights`, `attn`, `normed_post` and `hidden`) count: a program that leaves them out, or rounds other values in their place, can miss the bound.
Values may be sent and summed in bfloat16 or wider, within the bound.
No kernel may reach another device: no remote copies, remote signals or barrier semaphores. Data moves between devices by JAX's collectives and lax.ppermute only.
A program may use at most 128 MiB of HBM per device.

```python
import math
import jax
import jax.numpy as jnp
from jax import lax

D = 2560
H = 32
KVH = 8
HD = 128
FF = 9728
GROUP = 4
REQ = 384
MEANB = 3
MAXB = 64
PAGE = 128
SLOTS = 288
HOLDERS = 8


def pages_and_lengths(key):
    key = jax.random.fold_in(key, 5)
    keys = jax.random.split(key, 7)
    order = jax.random.permutation(keys[0], REQ).astype(jnp.int32)
    steps = jax.random.randint(keys[1], (REQ // 2,), 0, MEANB).astype(jnp.int32)
    delta = jnp.zeros((REQ,), jnp.int32).at[order[0::2]].set(steps).at[order[1::2]].set(-steps)
    counts = MEANB + delta
    forced = jax.random.randint(keys[2], (), 0, REQ)
    request_ids = jnp.arange(REQ, dtype=jnp.int32)
    counts = jnp.where(request_ids == forced, MAXB, counts)
    tails = jax.random.randint(keys[3], (REQ,), 1, PAGE + 1).astype(jnp.int32)
    tails = jnp.where(request_ids == forced, PAGE, tails)
    lengths = (counts - 1) * PAGE + tails
    blocks = jnp.arange(MAXB, dtype=jnp.int32)
    valid = (blocks[None, :] < counts[:, None]).reshape(-1).astype(jnp.int32)
    visit = jax.random.permutation(keys[4], REQ * MAXB).astype(jnp.int32)
    running = jnp.cumsum(valid[visit]) - 1
    rank = jnp.zeros((REQ * MAXB,), jnp.int32).at[visit].set(running.astype(jnp.int32))
    busy = jax.random.randint(keys[5], (), 0, HOLDERS)
    later = jnp.maximum(rank - SLOTS, 0)
    other = later % (HOLDERS - 1)
    holder = jnp.where(rank < SLOTS, busy, other + (other >= busy).astype(jnp.int32))
    slot = jnp.where(rank < SLOTS, rank, later // (HOLDERS - 1))
    slot = jnp.clip(slot, 0, SLOTS - 1)
    shuffle = jax.vmap(lambda sub_key: jax.random.permutation(sub_key, SLOTS))(jax.random.split(keys[6], HOLDERS)).astype(jnp.int32)
    placed = holder * SLOTS + shuffle[holder, slot]
    table = jnp.where(valid == 1, placed, -1).reshape(REQ, MAXB)
    return (lengths.astype(jnp.int32), table.astype(jnp.int32))


def draw_cache_len(key, part):
    return pages_and_lengths(key)[0]


def draw_page_table(key, part):
    return pages_and_lengths(key)[1]


def draw_key_cache(key, part):
    shape = (HOLDERS * SLOTS, KVH, PAGE, HD)
    base = jax.random.normal(key, shape, jnp.float32)
    return (base * 2.5).astype(jnp.bfloat16)


def spiked(drawn, rng, source, target, blocks, factor):
    def block_of(dim):
        return (jnp.arange(drawn.shape[dim]) // (drawn.shape[dim] // blocks)).reshape((-1,) + (1,) * (drawn.ndim - 1 - dim))

    first = jax.random.permutation(rng, blocks)[block_of(target)]
    second = (block_of(target) + blocks // 2) % blocks
    return jnp.where((block_of(source) == first) | (block_of(source) == second), factor * drawn, drawn)


def block_levels(key, extent, cuts, least, largest):
    factor_of = 1.0
    for dim, parts in cuts:
        draws = jax.random.uniform(jax.random.fold_in(jax.random.fold_in(key, 6), dim), (parts,), jnp.float32, least / len(cuts), largest / len(cuts))
        factor_of = factor_of * jnp.repeat(jnp.exp(draws), extent[dim] // parts).reshape((-1,) + (1,) * (len(extent) - 1 - dim))
    return factor_of


def bell_draw(key, dims, width, bound, cuts=(), kind=jnp.bfloat16):
    entries = width * jax.random.normal(key, dims, jnp.float32)
    if cuts:
        entries = entries * block_levels(key, dims, cuts, -0.22, 0.18)
    return jnp.clip(entries, -bound, bound).astype(kind)


def noise_with(stream_key, dims, spread, limit, cuts, heavy, held_as=jnp.bfloat16):
    values = spread * jax.random.normal(stream_key, dims, jnp.float32)
    if cuts:
        values = values * block_levels(stream_key, dims, cuts, -0.22, 0.18)
    return jnp.clip(spiked(values, jax.random.fold_in(stream_key, 3), *heavy), -limit, limit).astype(held_as)


def setup_inputs(seed: int = 0) -> dict:
    seeds = jax.random.split(jax.random.key(seed), 14)
    states = bell_draw(seeds[0], (REQ, D), 0.5, 3.0, ((0, 8),))
    gain_in = jnp.clip(1.0 + 0.18 * jax.random.normal(seeds[1], (D,), jnp.float32), 0.1, 1.9)
    w_qkv = bell_draw(seeds[2], (D, KVH, GROUP + 2, HD), D ** -0.5, 0.125, ((0, 2), (1, 8)))
    q_gain = jnp.clip(1.0 + 0.18 * jax.random.normal(seeds[3], (HD,), jnp.float32), 0.1, 1.9)
    k_gain = jnp.clip(1.0 + 0.18 * jax.random.normal(seeds[4], (HD,), jnp.float32), 0.1, 1.9)
    key_cache = draw_key_cache(jax.random.fold_in(seeds[13], 71), 0)
    value_cache = bell_draw(seeds[6], (HOLDERS * SLOTS, KVH, PAGE, HD), 2.0, 12.0, ((0, 8), (1, 8), (2, 2)))
    cache_len = draw_cache_len(jax.random.fold_in(seeds[13], 71), 0)
    page_table = draw_page_table(jax.random.fold_in(seeds[13], 71), 0)
    w_out = noise_with(seeds[9], (H * HD, D), (H * HD) ** -0.5, 0.125, ((0, 8),), (0, 1, 8, 2.0))
    gain_post = jnp.clip(1.0 + 0.18 * jax.random.normal(seeds[10], (D,), jnp.float32), 0.1, 1.9)
    w_gate_up = bell_draw(seeds[11], (D, 2, FF), D ** -0.5, 0.125, ((2, 16),))
    w_down = noise_with(seeds[12], (FF, D), FF ** -0.5, 0.078125, ((0, 16),), (0, 1, 16, 2.0))
    return {"states": states, "gain_in": gain_in, "w_qkv": w_qkv, "q_gain": q_gain, "k_gain": k_gain, "key_cache": key_cache, "value_cache": value_cache, "cache_len": cache_len, "page_table": page_table, "w_out": w_out, "gain_post": gain_post, "w_gate_up": w_gate_up, "w_down": w_down}


epsilon = 1e-06
rope_base = 1000000.0
masked_score = -1e+30

def rms_scale(values, gain):
    return values * lax.rsqrt(lax.optimization_barrier(jnp.mean(values * values, axis=-1, keepdims=True)) + epsilon) * gain

def rotate(values, angle_pos):
    half = values.shape[-1] // 2
    ramp = jnp.arange(half).astype(jnp.float32)
    freqs = jnp.exp(ramp * (-2.0 * math.log(rope_base) / values.shape[-1]))
    angle = angle_pos[..., None] * freqs
    cosine = jnp.cos(angle)
    sine = jnp.sin(angle)
    lower = values[..., :half]
    upper = values[..., half:]
    return jnp.concatenate([lower * cosine - upper * sine, upper * cosine + lower * sine], axis=-1)

def reference(states, gain_in, w_qkv, q_gain, k_gain, key_cache, value_cache, cache_len, page_table, w_out, gain_post, w_gate_up, w_down):
    scale = HD ** (-0.5)
    resid_in = states.astype(jnp.float32)
    normed = rms_scale(resid_in, gain_in).astype(jnp.bfloat16)
    proj = jnp.dot(normed, w_qkv.reshape(D, KVH * (GROUP + 2) * HD), preferred_element_type=jnp.float32)
    proj = proj.reshape(REQ, KVH, GROUP + 2, HD)
    position = cache_len.astype(jnp.float32)
    query = rotate(rms_scale(proj[:, :, :GROUP], q_gain), jnp.broadcast_to(position[:, None, None], (REQ, KVH, GROUP))).astype(jnp.bfloat16)
    key_new = rotate(rms_scale(proj[:, :, GROUP], k_gain), jnp.broadcast_to(position[:, None], (REQ, KVH))).astype(jnp.bfloat16)
    value_new = proj[:, :, GROUP + 1].astype(jnp.bfloat16)
    token_index = jnp.arange(MAXB * PAGE, dtype=jnp.int32)

    def attend(inputs):
        query_one, key_one, value_one, pages, length = inputs
        slot_ids = jnp.maximum(pages, 0)
        keys = jnp.swapaxes(key_cache[slot_ids], 0, 1).reshape(KVH, MAXB * PAGE, HD).astype(jnp.float32)
        values = jnp.swapaxes(value_cache[slot_ids], 0, 1).reshape(KVH, MAXB * PAGE, HD).astype(jnp.float32)
        query_full = query_one.astype(jnp.float32)
        scores = jnp.einsum('kgd,ktd->kgt', query_full, keys, precision=lax.Precision.HIGHEST) * scale
        live = (token_index < length)[None, None, :]
        scores = jnp.where(live, scores, masked_score)
        own_score = jnp.einsum('kgd,kd->kg', query_full, key_one.astype(jnp.float32), precision=lax.Precision.HIGHEST) * scale
        top = jnp.maximum(lax.optimization_barrier(jnp.max(scores, axis=-1)), own_score)
        expo = jnp.where(live, jnp.exp(scores - top[..., None]), 0.0)
        own_expo = jnp.exp(own_score - top)
        total = lax.optimization_barrier(jnp.sum(expo, axis=-1)) + own_expo
        weights = lax.optimization_barrier(expo.astype(jnp.bfloat16)).astype(jnp.float32)
        own_weight = lax.optimization_barrier(own_expo.astype(jnp.bfloat16)).astype(jnp.float32)
        summed = jnp.einsum('kgt,ktd->kgd', weights, values, precision=lax.Precision.HIGHEST)
        summed = summed + own_weight[..., None] * value_one.astype(jnp.float32)[:, None, :]
        return (summed / total[..., None]).astype(jnp.bfloat16)
    attn = lax.map(attend, (query, key_new, value_new, page_table, cache_len)).reshape(REQ, H * HD)
    mixed = jnp.dot(attn, w_out, preferred_element_type=jnp.float32)
    resid = resid_in + mixed
    normed_post = rms_scale(resid, gain_post).astype(jnp.bfloat16)
    gate_up = jnp.dot(normed_post, w_gate_up.reshape(D, 2 * FF), preferred_element_type=jnp.float32).reshape(REQ, 2, FF)
    hidden = (jax.nn.silu(gate_up[:, 0]) * gate_up[:, 1]).astype(jnp.bfloat16)
    down = jnp.dot(hidden, w_down, preferred_element_type=jnp.float32)
    return (mixed.astype(jnp.bfloat16), (resid + down).astype(jnp.bfloat16))
```

```python
import functools
import math

import jax
import jax.numpy as jnp
from jax import lax
from jax.experimental import pallas as pl
from jax.experimental.pallas import tpu as pltpu
from jax.sharding import PartitionSpec as P

epsilon = 1e-06
rope_base = 1000000.0
masked_score = -1e30
lane = 128
unit_pad = 64
short_pages = 5
code_span = 128
f32 = jnp.float32
bf16 = jnp.bfloat16


def call(kernel, out_shapes, operands, scratch=(), scalars=0, limit=24):
    smem = pl.BlockSpec(memory_space=pltpu.SMEM)
    vmem = pl.BlockSpec(memory_space=pltpu.VMEM)
    single = isinstance(out_shapes, tuple)
    outs = [out_shapes] if single else out_shapes
    result = pl.pallas_call(
        kernel,
        out_shape=[jax.ShapeDtypeStruct(*o) for o in outs],
        in_specs=[smem] * scalars + [vmem] * (len(operands) - scalars),
        out_specs=[vmem] * len(outs),
        scratch_shapes=list(scratch),
        compiler_params=pltpu.CompilerParams(vmem_limit_bytes=limit << 20),
    )(*operands)
    return result[0] if single else result


def exchange(blocks, axes):
    return lax.all_to_all(blocks, axes, split_axis=0, concat_axis=0, tiled=True)


def project_kernel(n_ref, states_ref, gain_ref, w_ref, out_ref, normed_ref):
    parts, part_width, head_dim = w_ref.shape
    x = states_ref[...].astype(f32)
    inverse = lax.rsqrt(jnp.mean(x * x, axis=-1, keepdims=True) + epsilon)
    normed_ref[...] = (x * inverse * gain_ref[...]).astype(bf16)
    start = pl.multiple_of(n_ref[0] * part_width, lane)
    own = normed_ref[:, pl.ds(start, part_width)]
    for c in range(parts):
        out_ref[:, c * head_dim : (c + 1) * head_dim] = jnp.dot(
            own, w_ref[c], preferred_element_type=f32
        )


def query_kernel(own_ref, other_ref, cos_ref, sin_ref, qg_ref, kg_ref, rows_ref, send_ref):
    head_dim = cos_ref.shape[1]
    copies, _, width = send_ref.shape
    group = width // head_dim
    proj = own_ref[...] + other_ref[...]
    cosine, sine = cos_ref[...], sin_ref[...]
    for c in range(group + 1):
        u = proj[:, c * head_dim : (c + 1) * head_dim]
        gain = qg_ref[...] if c < group else kg_ref[...]
        u = u * lax.rsqrt(jnp.mean(u * u, axis=-1, keepdims=True) + epsilon) * gain
        v = (u * cosine + pltpu.roll(u, head_dim // 2, 1) * sine).astype(bf16)
        rows_ref[:, c * head_dim : (c + 1) * head_dim] = v.astype(f32)
        if c < group:
            for d in range(copies):
                send_ref[d, :, c * head_dim : (c + 1) * head_dim] = v
    c = group + 1
    rows_ref[:, c * head_dim : (c + 1) * head_dim] = (
        proj[:, c * head_dim : (c + 1) * head_dim].astype(bf16).astype(f32)
    )


def slot_kernel(p_ref, n_ref, pages_ref, len_ref, member_ref, count_ref, owner_ref):
    slot_count, req_count = member_ref.shape
    max_blocks = pages_ref.shape[0]
    half_page = code_span // 2
    first_slot = (p_ref[0] * slot_count).astype(f32)
    first_token = (n_ref[0] * half_page).astype(f32)
    lengths = len_ref[...].astype(f32)
    pages = pages_ref[...].astype(f32)
    request = lax.broadcasted_iota(jnp.int32, (1, req_count), 1).astype(f32)
    slot = lax.broadcasted_iota(jnp.int32, (slot_count, 1), 0).astype(f32) + first_slot
    code = jnp.full((slot_count, req_count), -1.0, f32)
    for b in range(short_pages):
        live = jnp.clip(lengths - (b * code_span) - first_token, 0.0, float(half_page))
        code = jnp.where(pages[b : b + 1] == slot, request * code_span + live, code)
    code = jnp.max(code, axis=1, keepdims=True)
    length = jnp.max(lengths, axis=1, keepdims=True)
    longest = lengths == length
    number = jnp.sum(jnp.where(longest, request, 0.0), axis=1, keepdims=True)
    column = jnp.sum(jnp.where(longest, pages, 0.0), axis=1, keepdims=True)
    column = jnp.concatenate(
        [column, jnp.full((lane - max_blocks, 1), -1.0, f32)], axis=0
    )
    row = jnp.transpose(jnp.broadcast_to(column, (lane, lane)))[:1]
    block = lax.broadcasted_iota(jnp.int32, (1, lane), 1).astype(f32)
    live = jnp.clip(length - block * code_span - first_token, 0.0, float(half_page))
    found = jnp.where(row == slot, number * code_span + live, -1.0)
    code = jnp.maximum(code, jnp.max(found, axis=1, keepdims=True))
    owner = jnp.floor(code * (1.0 / code_span))
    count_ref[...] = jnp.broadcast_to(
        jnp.where(code >= 0, code - owner * code_span, 0.0), count_ref.shape
    )
    member_ref[...] = jnp.where(owner == request, 1.0, 0.0).astype(bf16)
    padded = owner_ref.shape[1]
    wide = jnp.broadcast_to(owner, (slot_count, lane))
    wide = jnp.concatenate([wide, jnp.full((padded - slot_count, lane), -1.0, f32)], axis=0)
    owner_ref[...] = jnp.transpose(wide)[: owner_ref.shape[0]]


def attend_kernel(
    q_ref,
    k_ref,
    v_ref,
    member_ref,
    count_ref,
    owner_ref,
    out_ref,
    qs_ref,
    o_ref,
    ml_ref,
    req_ref,
):
    slot_count, half_page, head_dim = k_ref.shape
    req_count = member_ref.shape[1]
    padded = ml_ref.shape[0]
    group = o_ref.shape[0]
    peers = out_ref.shape[0]
    rows = req_count // peers
    scale = head_dim ** (-0.5)
    block = 8
    queries = q_ref[...].reshape(req_count, group * head_dim)
    qs_ref[...] = jnp.dot(member_ref[...], queries, preferred_element_type=f32)
    columns = block * half_page
    relative = lax.broadcasted_iota(jnp.int32, (block, columns), 1) - (
        half_page * lax.broadcasted_iota(jnp.int32, (block, columns), 0)
    )
    relative = relative.astype(f32)
    positive = relative >= 0.0
    spot = lax.broadcasted_iota(jnp.int32, (block, lane), 1)
    o_ref[:, slot_count:, :] = jnp.zeros((group, padded - slot_count, head_dim), bf16)
    ml_ref[slot_count:, :] = jnp.where(
        lax.broadcasted_iota(jnp.int32, (padded - slot_count, lane), 1) < group, masked_score, 0.0
    )

    def step(i, carry):
        outs = []
        for half in range(2):
            base = pl.multiple_of(i * (2 * block) + half * block, block)
            qb = qs_ref[pl.ds(base, block), :]
            q = jnp.concatenate(
                [qb[:, g * head_dim : (g + 1) * head_dim] for g in range(group)], axis=0
            ).astype(bf16)
            k = k_ref[pl.ds(base, block)].reshape(columns, head_dim)
            v = v_ref[pl.ds(base, block)].reshape(columns, head_dim)
            s = lax.dot_general(q, k, (((1,), (1,)), ((), ())), preferred_element_type=f32)
            s = s.reshape(group, block, columns) * scale
            count = count_ref[pl.ds(base, block), :1]
            live = (positive & (relative < count))[None]
            s = jnp.where(live, s, masked_score)
            top = jnp.max(s, axis=-1, keepdims=True)
            p = jnp.where(live, jnp.exp(s - top), 0.0)
            total = jnp.sum(p, axis=-1, keepdims=True)
            o = jnp.dot(
                p.reshape(group * block, columns).astype(bf16), v, preferred_element_type=f32
            )
            outs.append(o.reshape(group, block, head_dim))
            stat = jnp.zeros((block, lane), f32)
            for g in range(group):
                stat = jnp.where(spot == g, top[g], stat)
                stat = jnp.where(spot == group + g, total[g], stat)
            ml_ref[pl.ds(base, block), :] = stat
        base = pl.multiple_of(i * (2 * block), 2 * block)
        o_ref[:, pl.ds(base, 2 * block), :] = jnp.concatenate(outs, axis=1).astype(bf16)
        return carry

    lax.fori_loop(0, slot_count // (2 * block), step, 0, unroll=2)

    stats = jnp.transpose(ml_ref[...])
    request = lax.broadcasted_iota(jnp.int32, (req_count, 1), 0).astype(f32)
    member = request == owner_ref[:1, :]
    spot = lax.broadcasted_iota(jnp.int32, (req_count, lane), 1)
    summary = jnp.zeros((req_count, lane), f32)
    for g in range(group):
        tops = jnp.where(member, stats[g : g + 1], masked_score)
        top = jnp.max(tops, axis=1, keepdims=True)
        weight = jnp.where(member, jnp.exp(tops - top), 0.0)
        total = jnp.sum(weight * stats[group + g : group + g + 1], axis=1, keepdims=True)
        req_ref[g] = jnp.dot(weight.astype(bf16), o_ref[g], preferred_element_type=f32)
        summary = jnp.where(spot == g, top, summary)
        summary = jnp.where(spot == group + g, total, summary)
    high = summary.astype(bf16).astype(f32)
    left = summary - high
    middle = left.astype(bf16).astype(f32)
    low = (left - middle).astype(bf16).astype(f32)
    req_ref[group] = (
        high + pltpu.roll(middle, 2 * group, 1) + pltpu.roll(low, 4 * group, 1)
    )
    blank = jnp.zeros((out_ref.shape[1] - (group + 1) * rows, lane), f32)
    for d in range(peers):
        pieces = [req_ref[g, d * rows : (d + 1) * rows, :] for g in range(group + 1)]
        out_ref[d] = jnp.concatenate(pieces + [blank], axis=0).astype(bf16)


def write_units(units_ref, values, out_ref, first, step, parts, units):
    rows, width = values.shape
    for c in range(width // lane):
        units_ref[c * rows : (c + 1) * rows, :] = values[:, c * lane : (c + 1) * lane]
    for w in range(parts):
        out_ref[first + step * w] = units_ref[w * units : w * units + unit_pad, :].astype(bf16)


def combine_kernel(n_ref, got_ref, rows_ref, w_ref, out_ref, units_ref):
    peers = got_ref.shape[0]
    group = w_ref.shape[0] // lane
    rows = rows_ref.shape[0] // 2
    parts = out_ref.shape[0]
    units = rows * w_ref.shape[1] // lane // parts
    scale = lane ** (-0.5)
    own = rows_ref[pl.ds(pl.multiple_of(n_ref[0] * rows, 8), rows), :]
    key = own[:, group * lane : (group + 1) * lane]
    value = own[:, (group + 1) * lane : (group + 2) * lane]
    spot = lax.broadcasted_iota(jnp.int32, (rows, lane), 1)
    own_score = jnp.full((rows, lane), masked_score, f32)
    for g in range(group):
        score = jnp.sum(own[:, g * lane : (g + 1) * lane] * key, axis=1, keepdims=True) * scale
        own_score = jnp.where(spot == g, score, own_score)
    top = own_score
    stats = []
    for d in range(peers):
        packed = got_ref[d, group * rows : (group + 2) * rows, :].astype(f32)[:rows]
        stat = (
            packed
            + pltpu.roll(packed, lane - 2 * group, 1)
            + pltpu.roll(packed, lane - 4 * group, 1)
        )
        stats.append(stat)
        top = jnp.maximum(top, jnp.where(spot < group, stat, masked_score))
    own_expo = jnp.exp(own_score - top)
    total = own_expo
    sums = [
        own_expo[:, g : g + 1].astype(bf16).astype(f32) * value for g in range(group)
    ]
    for d in range(peers):
        factor = jnp.where(spot < group, jnp.exp(stats[d] - top), 0.0)
        total = total + factor * pltpu.roll(stats[d], lane - group, 1)
        got = got_ref[d].astype(f32)
        for g in range(group):
            sums[g] = sums[g] + factor[:, g : g + 1] * got[g * rows : (g + 1) * rows]
    attn = jnp.concatenate(
        [(sums[g] / total[:, g : g + 1]).astype(bf16) for g in range(group)], axis=1
    )
    mixed = jnp.dot(attn, w_ref[...], preferred_element_type=f32)
    units_ref[rows * mixed.shape[1] // lane :, :] = jnp.zeros((8, lane), f32)
    write_units(units_ref, mixed, out_ref, 0, 1, parts, units)


def residual_kernel(w_ref, n_ref, got_ref, states_ref, send_ref, resid_ref, units_ref):
    parts = got_ref.shape[0]
    rows = states_ref.shape[0] // 2
    width = states_ref.shape[1]
    units = rows * width // lane // parts
    mixed = got_ref[0].astype(f32)
    for w in range(1, parts):
        mixed = mixed + got_ref[w].astype(f32)
    for d in range(send_ref.shape[0]):
        send_ref[d] = mixed.astype(bf16)
    states = states_ref[...].astype(f32)
    states = jnp.where(n_ref[0] == 0, states[:rows], states[rows:])
    for c in range(width // lane):
        units_ref[c * rows : (c + 1) * rows, :] = states[:, c * lane : (c + 1) * lane]
    units_ref[rows * width // lane :, :] = jnp.zeros((8, lane), f32)
    for w in range(parts):

        @pl.when(w_ref[0] == w)
        def _():
            resid_ref[...] = mixed + units_ref[w * units : w * units + unit_pad, :]


def read_units(got_ref, units_ref, parts, units):
    for w in range(parts):
        for n in range(2):
            units_ref[n, w * units : (w + 1) * units, :] = got_ref[2 * w + n].astype(f32)[:units]


def hidden_kernel(
    got_ref, states_ref, gain_ref, wg_ref, wd_ref, mixed_ref, out_ref, units_ref, x_ref, flat_ref
):
    rows, width = states_ref.shape
    half = rows // 2
    parts = got_ref.shape[0] // 2
    units = half * width // lane // parts
    read_units(got_ref, units_ref, parts, units)
    square = jnp.zeros((rows, lane), f32)
    for c in range(width // lane):
        span = slice(c * lane, (c + 1) * lane)
        mixed = jnp.concatenate(
            [units_ref[n, c * half : (c + 1) * half, :] for n in range(2)], axis=0
        )
        mixed_ref[:, span] = mixed.astype(bf16)
        resid = states_ref[:, span].astype(f32) + mixed
        x_ref[:, span] = resid
        square = square + resid * resid
    inverse = lax.rsqrt(jnp.sum(square, axis=1, keepdims=True) * (1.0 / width) + epsilon)
    normed = (x_ref[...] * inverse * gain_ref[...]).astype(bf16)
    contract = (((1,), (1,)), ((), ()))
    gate = lax.dot_general(normed, wg_ref[0], contract, preferred_element_type=f32)
    up = lax.dot_general(normed, wg_ref[1], contract, preferred_element_type=f32)
    hidden = (gate / (1.0 + jnp.exp(-gate)) * up).astype(bf16)
    down = jnp.dot(hidden, wd_ref[...], preferred_element_type=f32)
    flat_ref[half * width // lane :, :] = jnp.zeros((8, lane), f32)
    for n in range(2):
        write_units(flat_ref, down[n * half : (n + 1) * half], out_ref, n, 2, parts, units)


def total_kernel(got_ref, resid_ref, send_ref):
    out = got_ref[0].astype(f32)
    for d in range(1, got_ref.shape[0]):
        out = out + got_ref[d].astype(f32)
    out = (resid_ref[...] + out).astype(bf16)
    for d in range(send_ref.shape[0]):
        send_ref[d] = out


def gather_kernel(got_ref, out_ref, units_ref):
    rows, width = out_ref.shape
    half = rows // 2
    parts = got_ref.shape[0] // 2
    units = half * width // lane // parts
    read_units(got_ref, units_ref, parts, units)
    for c in range(width // lane):
        block = jnp.concatenate(
            [units_ref[n, c * half : (c + 1) * half, :] for n in range(2)], axis=0
        )
        out_ref[:, c * lane : (c + 1) * lane] = block.astype(bf16)


def per_device(
    states,
    gain_in,
    w_qkv,
    q_gain,
    k_gain,
    key_cache,
    value_cache,
    cache_len,
    page_table,
    w_out,
    gain_post,
    w_gate_up,
    w_down,
):
    parts = w_qkv.shape[2]
    group = parts - 2
    head_dim = w_qkv.shape[3]
    narrow_size = lax.axis_size("narrow")
    wide_size = lax.axis_size("wide")
    holders = lax.axis_size("pool")
    peers = holders * narrow_size
    split = wide_size * narrow_size
    narrow = lax.axis_index("narrow").reshape(1)
    wide = lax.axis_index("wide").reshape(1)
    pool = lax.axis_index("pool").reshape(1)
    rows, width = states.shape
    half = rows // narrow_size
    req_count = page_table.shape[0]
    slot_count = key_cache.shape[0]
    half_page = key_cache.shape[2]
    keys = key_cache.reshape(slot_count, half_page, head_dim)
    values = value_cache.reshape(slot_count, half_page, head_dim)
    slot_pad = -(-slot_count // lane) * lane
    half_units = half * width // lane

    partial_proj = call(
        project_kernel,
        ((rows, parts * head_dim), f32),
        [narrow, states, gain_in[None], w_qkv[:, 0].swapaxes(0, 1)],
        [pltpu.VMEM((rows, width), bf16)],
        scalars=1,
    )
    swap = [(i, narrow_size - 1 - i) for i in range(narrow_size)]
    other_proj = lax.ppermute(partial_proj, "narrow", swap)
    own_len = lax.dynamic_slice_in_dim(cache_len, pool[0] * rows, rows, 0).astype(f32)
    ramp = jnp.arange(head_dim // 2).astype(f32)
    freqs = jnp.exp(ramp * (-2.0 * math.log(rope_base) / head_dim))
    angle = own_len[:, None] * freqs
    cosine, sine = jnp.cos(angle), jnp.sin(angle)
    cosine = jnp.concatenate([cosine, cosine], axis=1)
    sine = jnp.concatenate([-sine, sine], axis=1)
    member, count, owner = call(
        slot_kernel,
        [
            ((slot_count, req_count), bf16),
            ((slot_count, lane), f32),
            ((8, slot_pad), f32),
        ],
        [pool, narrow, page_table.T, cache_len[None]],
        scalars=2,
    )
    qkv_rows, sent = call(
        query_kernel,
        [((rows, parts * head_dim), f32), ((holders, rows, group * head_dim), bf16)],
        [partial_proj, other_proj, cosine, sine, q_gain[None], k_gain[None]],
    )
    queries = exchange(sent, "pool")
    payload = call(
        attend_kernel,
        ((peers, lane, lane), bf16),
        [queries, keys, values, member, count, owner],
        [
            pltpu.VMEM((slot_count, group * head_dim), f32),
            pltpu.VMEM((group, slot_pad, head_dim), bf16),
            pltpu.VMEM((slot_pad, lane), f32),
            pltpu.VMEM((group + 1, req_count, head_dim), f32),
        ],
    )
    got = exchange(payload, ("pool", "narrow"))
    sent = call(
        combine_kernel,
        ((wide_size, unit_pad, lane), bf16),
        [narrow, got, qkv_rows, w_out],
        [pltpu.VMEM((half_units + 8, lane), f32)],
        scalars=1,
    )
    got = exchange(sent, "wide")
    sent, resid_units = call(
        residual_kernel,
        [((split, unit_pad, lane), bf16), ((unit_pad, lane), f32)],
        [wide, narrow, got, states],
        [pltpu.VMEM((half_units + 8, lane), f32)],
        scalars=2,
    )
    both = ("wide", "narrow")
    got = exchange(sent, both)
    attn_mixed, sent = call(
        hidden_kernel,
        [((rows, width), bf16), ((split, unit_pad, lane), bf16)],
        [got, states, gain_post[None], w_gate_up.transpose(1, 2, 0), w_down],
        [
            pltpu.VMEM((narrow_size, half_units, lane), f32),
            pltpu.VMEM((rows, width), f32),
            pltpu.VMEM((half_units + 8, lane), f32),
        ],
    )
    got = exchange(sent, both)
    sent = call(total_kernel, ((split, unit_pad, lane), bf16), [got, resid_units])
    got = exchange(sent, both)
    layer_out = call(
        gather_kernel,
        ((rows, width), bf16),
        [got],
        [pltpu.VMEM((narrow_size, half_units, lane), f32)],
    )
    return (attn_mixed, layer_out)


def solution(mesh):
    in_specs = (
        P("pool", None),
        P(),
        P("narrow", "wide", None, None),
        P(),
        P(),
        P("pool", "wide", "narrow", None),
        P("pool", "wide", "narrow", None),
        P(),
        P(),
        P("wide", None),
        P(),
        P(None, None, ("wide", "narrow")),
        P(("wide", "narrow"), None),
    )
    out_specs = (P("pool", None), P("pool", None))
    return jax.shard_map(
        per_device, mesh=mesh, in_specs=in_specs, out_specs=out_specs, check_vma=False
    )
```

```python
import functools
import math

import jax
import jax.numpy as jnp
from jax import lax
from jax.experimental import pallas as pl
from jax.experimental.pallas import tpu as pltpu
from jax.sharding import PartitionSpec as P

epsilon = 1e-06
rope_base = 1000000.0
masked_score = -1e30
lane = 128
unit_pad = 64
short_pages = 5
code_span = 128
f32 = jnp.float32
bf16 = jnp.bfloat16


def call(kernel, out_shapes, operands, scratch=(), scalars=0, limit=24, in_place=()):
    spaces = [pltpu.SMEM] * scalars + [pltpu.VMEM] * (len(operands) - scalars)
    for i in in_place:
        spaces[i] = pltpu.HBM
    operands = [
        pltpu.with_memory_space_constraint(x, pltpu.HBM) if i in in_place else x
        for i, x in enumerate(operands)
    ]
    single = isinstance(out_shapes, tuple)
    outs = [out_shapes] if single else out_shapes
    result = pl.pallas_call(
        kernel,
        out_shape=[jax.ShapeDtypeStruct(*o) for o in outs],
        in_specs=[pl.BlockSpec(memory_space=space) for space in spaces],
        out_specs=[pl.BlockSpec(memory_space=pltpu.VMEM)] * len(outs),
        scratch_shapes=list(scratch),
        compiler_params=pltpu.CompilerParams(vmem_limit_bytes=limit << 20),
    )(*operands)
    return result[0] if single else result


def place(index_ref):
    index = index_ref[0]
    return index // 16, index // 2 % 8, index % 2


def exchange(blocks, axes):
    return lax.all_to_all(blocks, axes, split_axis=0, concat_axis=0, tiled=True)


def project_kernel(
    index_ref,
    states_hbm,
    gain_hbm,
    w_hbm,
    qg_hbm,
    kg_hbm,
    out_ref,
    gains_ref,
    states_ref,
    gain_ref,
    w_ref,
    normed_ref,
    sems,
):
    parts, part_width, head_dim = w_ref.shape
    width = states_ref.shape[1]
    copies = [
        pltpu.make_async_copy(states_hbm, states_ref, sems.at[0]),
        pltpu.make_async_copy(gain_hbm, gain_ref, sems.at[1]),
        pltpu.make_async_copy(qg_hbm, gains_ref.at[0], sems.at[2]),
        pltpu.make_async_copy(kg_hbm, gains_ref.at[1], sems.at[3]),
    ]
    weights = [
        pltpu.make_async_copy(w_hbm.at[c], w_ref.at[c], sems.at[4 + c]) for c in range(parts)
    ]
    for copy in copies + weights:
        copy.start()
    copies[0].wait()
    square = jnp.zeros((states_ref.shape[0], lane), f32)
    for c in range(width // lane):
        x = states_ref[:, c * lane : (c + 1) * lane].astype(f32)
        square = square + x * x
    inverse = lax.rsqrt(jnp.sum(square, axis=1, keepdims=True) * (1.0 / width) + epsilon)
    copies[1].wait()
    for c in range(width // lane):
        span = slice(c * lane, (c + 1) * lane)
        x = states_ref[:, span].astype(f32)
        normed_ref[:, span] = (x * inverse * gain_ref[c : c + 1, :]).astype(bf16)
    narrow = place(index_ref)[2]
    own = normed_ref[:, pl.ds(pl.multiple_of(narrow * part_width, lane), part_width)]
    for c in range(parts):
        weights[c].wait()
        out_ref[:, c * head_dim : (c + 1) * head_dim] = jnp.dot(
            own, w_ref[c], preferred_element_type=f32
        )
    copies[2].wait()
    copies[3].wait()


def query_kernel(own_ref, other_ref, cos_ref, sin_ref, gains_ref, first_ref, rows_ref, send_ref):
    head_dim = cos_ref.shape[1]
    copies, _, width = send_ref.shape
    group = width // head_dim
    proj = own_ref[...] + other_ref[...]
    cosine, sine = cos_ref[...], sin_ref[...]
    for c in range(group + 1):
        u = proj[:, c * head_dim : (c + 1) * head_dim]
        gain = gains_ref[0:1, :] if c < group else gains_ref[1:2, :]
        u = u * lax.rsqrt(jnp.mean(u * u, axis=-1, keepdims=True) + epsilon) * gain
        v = (u * cosine + pltpu.roll(u, head_dim // 2, 1) * sine).astype(bf16)
        rows_ref[:, c * head_dim : (c + 1) * head_dim] = v.astype(f32)
        if c < group:
            for d in range(copies):
                send_ref[d, :, c * head_dim : (c + 1) * head_dim] = v
    c = group + 1
    rows_ref[:, c * head_dim : (c + 1) * head_dim] = (
        proj[:, c * head_dim : (c + 1) * head_dim].astype(bf16).astype(f32)
    )


def slot_kernel(
    index_ref, pages_hbm, len_hbm, member_ref, count_ref, owner_ref, pages_ref, len_ref, sems
):
    copies = [
        pltpu.make_async_copy(pages_hbm, pages_ref, sems.at[0]),
        pltpu.make_async_copy(len_hbm, len_ref.at[0], sems.at[1]),
    ]
    for copy in copies:
        copy.start()
    for copy in copies:
        copy.wait()
    slot_count, req_count = member_ref.shape
    max_blocks = pages_ref.shape[0]
    half_page = code_span // 2
    pool, _, narrow = place(index_ref)
    first_slot = (pool * slot_count).astype(f32)
    first_token = (narrow * half_page).astype(f32)
    lengths = len_ref[...].astype(f32)
    pages = pages_ref[...].astype(f32)
    request = lax.broadcasted_iota(jnp.int32, (1, req_count), 1).astype(f32)
    slot = lax.broadcasted_iota(jnp.int32, (slot_count, 1), 0).astype(f32) + first_slot
    code = jnp.full((slot_count, req_count), -1.0, f32)
    for b in range(short_pages):
        live = jnp.clip(lengths - (b * code_span) - first_token, 0.0, float(half_page))
        code = jnp.where(pages[b : b + 1] == slot, request * code_span + live, code)
    code = jnp.max(code, axis=1, keepdims=True)
    length = jnp.max(lengths, axis=1, keepdims=True)
    longest = lengths == length
    number = jnp.sum(jnp.where(longest, request, 0.0), axis=1, keepdims=True)
    column = jnp.sum(jnp.where(longest, pages, 0.0), axis=1, keepdims=True)
    column = jnp.concatenate(
        [column, jnp.full((lane - max_blocks, 1), -1.0, f32)], axis=0
    )
    row = jnp.transpose(jnp.broadcast_to(column, (lane, lane)))[:1]
    block = lax.broadcasted_iota(jnp.int32, (1, lane), 1).astype(f32)
    live = jnp.clip(length - block * code_span - first_token, 0.0, float(half_page))
    found = jnp.where(row == slot, number * code_span + live, -1.0)
    code = jnp.maximum(code, jnp.max(found, axis=1, keepdims=True))
    owner = jnp.floor(code * (1.0 / code_span))
    count_ref[...] = jnp.broadcast_to(
        jnp.where(code >= 0, code - owner * code_span, 0.0), count_ref.shape
    )
    member_ref[...] = jnp.where(owner == request, 1.0, 0.0).astype(bf16)
    padded = owner_ref.shape[1]
    wide = jnp.broadcast_to(owner, (slot_count, lane))
    wide = jnp.concatenate([wide, jnp.full((padded - slot_count, lane), -1.0, f32)], axis=0)
    owner_ref[...] = jnp.transpose(wide)[: owner_ref.shape[0]]


def attend_kernel(
    q_ref,
    k_hbm,
    v_hbm,
    member_ref,
    count_ref,
    owner_ref,
    out_ref,
    k_ref,
    v_ref,
    qs_ref,
    o_ref,
    ml_ref,
    req_ref,
    sems,
):
    slot_count, half_page, head_dim = k_ref.shape
    req_count = member_ref.shape[1]
    padded = ml_ref.shape[0]
    group = o_ref.shape[0]
    peers = out_ref.shape[0]
    rows = req_count // peers
    chunks = sems.shape[1]
    chunk = slot_count // chunks
    scale = head_dim ** (-0.5)
    block = 8

    def copies(i):
        span = pl.ds(i * chunk, chunk)
        return (
            pltpu.make_async_copy(k_hbm.at[span], k_ref.at[span], sems.at[0, i]),
            pltpu.make_async_copy(v_hbm.at[span], v_ref.at[span], sems.at[1, i]),
        )

    for i in range(chunks):
        for copy in copies(i):
            copy.start()
    queries = q_ref[...].reshape(req_count, group * head_dim)
    qs_ref[...] = jnp.dot(member_ref[...], queries, preferred_element_type=f32)
    columns = block * half_page
    relative = lax.broadcasted_iota(jnp.int32, (block, columns), 1) - (
        half_page * lax.broadcasted_iota(jnp.int32, (block, columns), 0)
    )
    relative = jnp.where(relative >= 0, relative, columns).astype(f32)
    spot = lax.broadcasted_iota(jnp.int32, (block, lane), 1)
    o_ref[:, slot_count:, :] = jnp.zeros((group, padded - slot_count, head_dim), bf16)
    ml_ref[slot_count:, :] = jnp.where(
        lax.broadcasted_iota(jnp.int32, (padded - slot_count, lane), 1) < group, masked_score, 0.0
    )

    def step(i, carry):
        k_copy, v_copy = copies(i)
        k_copy.wait()
        bases = [pl.multiple_of(i * chunk + b * block, block) for b in range(chunk // block)]
        scores = []
        for base in bases:
            qb = qs_ref[pl.ds(base, block), :]
            q = jnp.concatenate(
                [qb[:, g * head_dim : (g + 1) * head_dim] for g in range(group)], axis=0
            ).astype(bf16)
            k = k_ref[pl.ds(base, block)].reshape(columns, head_dim)
            scores.append(
                lax.dot_general(q, k, (((1,), (1,)), ((), ())), preferred_element_type=f32)
            )
        weights, tops, totals = [], [], []
        for base, s in zip(bases, scores):
            s = s.reshape(group, block, columns) * scale
            live = (relative < count_ref[pl.ds(base, block), :1])[None]
            s = jnp.where(live, s, masked_score)
            top = jnp.max(s, axis=-1, keepdims=True)
            p = jnp.where(live, jnp.exp(s - top), 0.0)
            tops.append(top)
            totals.append(jnp.sum(p, axis=-1, keepdims=True))
            weights.append(p.reshape(group * block, columns).astype(bf16))
        v_copy.wait()
        outs = []
        for base, p in zip(bases, weights):
            v = v_ref[pl.ds(base, block)].reshape(columns, head_dim)
            o = jnp.dot(p, v, preferred_element_type=f32)
            outs.append(o.reshape(group, block, head_dim))
        for base, top, total in zip(bases, tops, totals):
            stat = jnp.zeros((block, lane), f32)
            for g in range(group):
                stat = jnp.where(spot == g, top[g], stat)
                stat = jnp.where(spot == group + g, total[g], stat)
            ml_ref[pl.ds(base, block), :] = stat
        first = pl.multiple_of(i * chunk, 2 * block)
        o_ref[:, pl.ds(first, chunk), :] = jnp.concatenate(outs, axis=1).astype(bf16)
        return carry

    lax.fori_loop(0, chunks, step, 0)

    stats = jnp.transpose(ml_ref[...])
    request = lax.broadcasted_iota(jnp.int32, (req_count, 1), 0).astype(f32)
    member = request == owner_ref[:1, :]
    spot = lax.broadcasted_iota(jnp.int32, (req_count, lane), 1)
    summary = jnp.zeros((req_count, lane), f32)
    for g in range(group):
        tops = jnp.where(member, stats[g : g + 1], masked_score)
        top = jnp.max(tops, axis=1, keepdims=True)
        weight = jnp.where(member, jnp.exp(tops - top), 0.0)
        total = jnp.sum(weight * stats[group + g : group + g + 1], axis=1, keepdims=True)
        req_ref[g] = jnp.dot(weight.astype(bf16), o_ref[g], preferred_element_type=f32)
        summary = jnp.where(spot == g, top, summary)
        summary = jnp.where(spot == group + g, total, summary)
    high = summary.astype(bf16).astype(f32)
    left = summary - high
    middle = left.astype(bf16).astype(f32)
    low = (left - middle).astype(bf16).astype(f32)
    req_ref[group] = (
        high + pltpu.roll(middle, 2 * group, 1) + pltpu.roll(low, 4 * group, 1)
    )
    for d in range(peers):
        pieces = [req_ref[g, d * rows : (d + 1) * rows, :] for g in range(group + 1)]
        out_ref[d] = jnp.concatenate(pieces, axis=0).astype(bf16)


def write_units(units_ref, values, out_ref, first, step, parts, units):
    rows, width = values.shape
    for c in range(width // lane):
        units_ref[c * rows : (c + 1) * rows, :] = values[:, c * lane : (c + 1) * lane]
    for w in range(parts):
        out_ref[first + step * w] = units_ref[w * units : w * units + unit_pad, :].astype(bf16)


def combine_kernel(index_ref, got_ref, rows_ref, w_ref, out_ref, units_ref):
    peers = got_ref.shape[0]
    group = w_ref.shape[0] // lane
    rows = rows_ref.shape[0] // 2
    parts = out_ref.shape[0]
    units = rows * w_ref.shape[1] // lane // parts
    scale = lane ** (-0.5)
    own = rows_ref[pl.ds(pl.multiple_of(place(index_ref)[2] * rows, 8), rows), :]
    key = own[:, group * lane : (group + 1) * lane]
    value = own[:, (group + 1) * lane : (group + 2) * lane]
    spot = lax.broadcasted_iota(jnp.int32, (rows, lane), 1)
    own_score = jnp.full((rows, lane), masked_score, f32)
    for g in range(group):
        score = jnp.sum(own[:, g * lane : (g + 1) * lane] * key, axis=1, keepdims=True) * scale
        own_score = jnp.where(spot == g, score, own_score)
    top = own_score
    stats = []
    for d in range(peers):
        packed = got_ref[d, group * rows :, :].astype(f32)
        stat = (
            packed
            + pltpu.roll(packed, lane - 2 * group, 1)
            + pltpu.roll(packed, lane - 4 * group, 1)
        )
        stats.append(stat)
        top = jnp.maximum(top, jnp.where(spot < group, stat, masked_score))
    own_expo = jnp.exp(own_score - top)
    total = own_expo
    sums = [
        own_expo[:, g : g + 1].astype(bf16).astype(f32) * value for g in range(group)
    ]
    for d in range(peers):
        factor = jnp.where(spot < group, jnp.exp(stats[d] - top), 0.0)
        total = total + factor * pltpu.roll(stats[d], lane - group, 1)
        got = got_ref[d].astype(f32)
        for g in range(group):
            sums[g] = sums[g] + factor[:, g : g + 1] * got[g * rows : (g + 1) * rows]
    attn = jnp.concatenate(
        [(sums[g] / total[:, g : g + 1]).astype(bf16) for g in range(group)], axis=1
    )
    mixed = jnp.dot(attn, w_ref[...], preferred_element_type=f32)
    units_ref[rows * mixed.shape[1] // lane :, :] = jnp.zeros((8, lane), f32)
    write_units(units_ref, mixed, out_ref, 0, 1, parts, units)


def residual_kernel(index_ref, got_ref, states_ref, send_ref, resid_ref, units_ref):
    parts = got_ref.shape[0]
    rows = states_ref.shape[0] // 2
    width = states_ref.shape[1]
    units = rows * width // lane // parts
    mixed = got_ref[0].astype(f32)
    for w in range(1, parts):
        mixed = mixed + got_ref[w].astype(f32)
    for d in range(send_ref.shape[0]):
        send_ref[d] = mixed.astype(bf16)
    states = states_ref[...].astype(f32)
    _, wide, narrow = place(index_ref)
    states = jnp.where(narrow == 0, states[:rows], states[rows:])
    for c in range(width // lane):
        units_ref[c * rows : (c + 1) * rows, :] = states[:, c * lane : (c + 1) * lane]
    units_ref[rows * width // lane :, :] = jnp.zeros((8, lane), f32)
    for w in range(parts):

        @pl.when(wide == w)
        def _():
            resid_ref[...] = mixed + units_ref[w * units : w * units + unit_pad, :]


def read_units(got_ref, units_ref, parts, units):
    for w in range(parts):
        for n in range(2):
            units_ref[n, w * units : (w + 1) * units, :] = got_ref[2 * w + n].astype(f32)[:units]


def hidden_kernel(
    got_ref,
    states_ref,
    gain_hbm,
    wg_ref,
    wd_ref,
    mixed_ref,
    out_ref,
    units_ref,
    x_ref,
    flat_ref,
    gain_ref,
    sem,
):
    rows, width = states_ref.shape
    half = rows // 2
    parts = got_ref.shape[0] // 2
    units = half * width // lane // parts
    gain_copy = pltpu.make_async_copy(gain_hbm, gain_ref, sem)
    gain_copy.start()
    read_units(got_ref, units_ref, parts, units)
    square = jnp.zeros((rows, lane), f32)
    for c in range(width // lane):
        span = slice(c * lane, (c + 1) * lane)
        mixed = jnp.concatenate(
            [units_ref[n, c * half : (c + 1) * half, :] for n in range(2)], axis=0
        )
        mixed_ref[:, span] = mixed.astype(bf16)
        resid = states_ref[:, span].astype(f32) + mixed
        x_ref[:, span] = resid
        square = square + resid * resid
    inverse = lax.rsqrt(jnp.sum(square, axis=1, keepdims=True) * (1.0 / width) + epsilon)
    gain_copy.wait()
    normed = jnp.concatenate(
        [
            (x_ref[:, c * lane : (c + 1) * lane] * inverse * gain_ref[c : c + 1, :]).astype(bf16)
            for c in range(width // lane)
        ],
        axis=1,
    )
    contract = (((1,), (1,)), ((), ()))
    gate = lax.dot_general(normed, wg_ref[0], contract, preferred_element_type=f32)
    up = lax.dot_general(normed, wg_ref[1], contract, preferred_element_type=f32)
    hidden = (gate / (1.0 + jnp.exp(-gate)) * up).astype(bf16)
    down = jnp.dot(hidden, wd_ref[...], preferred_element_type=f32)
    flat_ref[half * width // lane :, :] = jnp.zeros((8, lane), f32)
    for n in range(2):
        write_units(flat_ref, down[n * half : (n + 1) * half], out_ref, n, 2, parts, units)


def total_kernel(got_ref, resid_ref, send_ref):
    out = got_ref[0].astype(f32)
    for d in range(1, got_ref.shape[0]):
        out = out + got_ref[d].astype(f32)
    out = (resid_ref[...] + out).astype(bf16)
    for d in range(send_ref.shape[0]):
        send_ref[d] = out


def gather_kernel(got_ref, out_ref, units_ref):
    rows, width = out_ref.shape
    half = rows // 2
    parts = got_ref.shape[0] // 2
    units = half * width // lane // parts
    read_units(got_ref, units_ref, parts, units)
    for c in range(width // lane):
        block = jnp.concatenate(
            [units_ref[n, c * half : (c + 1) * half, :] for n in range(2)], axis=0
        )
        out_ref[:, c * lane : (c + 1) * lane] = block.astype(bf16)


def per_device(
    states,
    gain_in,
    w_qkv,
    q_gain,
    k_gain,
    key_cache,
    value_cache,
    cache_len,
    page_table,
    w_out,
    gain_post,
    w_gate_up,
    w_down,
):
    parts = w_qkv.shape[2]
    group = parts - 2
    head_dim = w_qkv.shape[3]
    narrow_size = lax.axis_size("narrow")
    wide_size = lax.axis_size("wide")
    holders = lax.axis_size("pool")
    peers = holders * narrow_size
    split = wide_size * narrow_size
    index = lax.axis_index(("pool", "wide", "narrow")).reshape(1)
    rows, width = states.shape
    half = rows // narrow_size
    req_count = page_table.shape[0]
    slot_count = key_cache.shape[0]
    half_page = key_cache.shape[2]
    keys = key_cache.reshape(slot_count, half_page, head_dim)
    values = value_cache.reshape(slot_count, half_page, head_dim)
    slot_pad = -(-slot_count // lane) * lane
    half_units = half * width // lane

    partial_proj, gains = call(
        project_kernel,
        [((rows, parts * head_dim), f32), ((2, head_dim), f32)],
        [index, states, gain_in.reshape(-1, lane), w_qkv[:, 0].swapaxes(0, 1), q_gain, k_gain],
        [
            pltpu.VMEM((rows, width), bf16),
            pltpu.VMEM((width // lane, lane), f32),
            pltpu.VMEM((parts, w_qkv.shape[0], head_dim), bf16),
            pltpu.VMEM((rows, width), bf16),
            pltpu.SemaphoreType.DMA((4 + parts,)),
        ],
        scalars=1,
        in_place=(1, 2, 3, 4, 5),
    )
    swap = [(i, narrow_size - 1 - i) for i in range(narrow_size)]
    other_proj = lax.ppermute(partial_proj, "narrow", swap)
    own_len = lax.dynamic_slice_in_dim(cache_len, lax.axis_index("pool") * rows, rows, 0).astype(f32)
    ramp = jnp.arange(head_dim // 2).astype(f32)
    freqs = jnp.exp(ramp * (-2.0 * math.log(rope_base) / head_dim))
    angle = own_len[:, None] * freqs
    cosine, sine = jnp.cos(angle), jnp.sin(angle)
    cosine = jnp.concatenate([cosine, cosine], axis=1)
    sine = jnp.concatenate([-sine, sine], axis=1)
    member, count, owner = call(
        slot_kernel,
        [
            ((slot_count, req_count), bf16),
            ((slot_count, lane), f32),
            ((8, slot_pad), f32),
        ],
        [index, page_table.T, cache_len],
        [
            pltpu.VMEM((page_table.shape[1], req_count), jnp.int32),
            pltpu.VMEM((1, req_count), jnp.int32),
            pltpu.SemaphoreType.DMA((2,)),
        ],
        scalars=1,
        in_place=(1, 2),
    )
    qkv_rows, sent = call(
        query_kernel,
        [((rows, parts * head_dim), f32), ((holders, rows, group * head_dim), bf16)],
        [partial_proj, other_proj, cosine, sine, gains, owner],
    )
    queries = exchange(sent, "pool")
    payload = call(
        attend_kernel,
        ((peers, (group + 1) * half, lane), bf16),
        [queries, keys, values, member, count, owner],
        [
            pltpu.VMEM(keys.shape, bf16),
            pltpu.VMEM(values.shape, bf16),
            pltpu.VMEM((slot_count, group * head_dim), f32),
            pltpu.VMEM((group, slot_pad, head_dim), bf16),
            pltpu.VMEM((slot_pad, lane), f32),
            pltpu.VMEM((group + 1, req_count, head_dim), f32),
            pltpu.SemaphoreType.DMA((2, 3)),
        ],
        in_place=(1, 2),
        limit=32,
    )
    got = exchange(payload, ("pool", "narrow"))
    sent = call(
        combine_kernel,
        ((wide_size, unit_pad, lane), bf16),
        [index, got, qkv_rows, w_out],
        [pltpu.VMEM((half_units + 8, lane), f32)],
        scalars=1,
    )
    got = exchange(sent, "wide")
    sent, resid_units = call(
        residual_kernel,
        [((split, unit_pad, lane), bf16), ((unit_pad, lane), f32)],
        [index, got, states],
        [pltpu.VMEM((half_units + 8, lane), f32)],
        scalars=1,
    )
    both = ("wide", "narrow")
    got = exchange(sent, both)
    attn_mixed, sent = call(
        hidden_kernel,
        [((rows, width), bf16), ((split, unit_pad, lane), bf16)],
        [got, states, gain_post.reshape(-1, lane), w_gate_up.transpose(1, 2, 0), w_down],
        [
            pltpu.VMEM((narrow_size, half_units, lane), f32),
            pltpu.VMEM((rows, width), f32),
            pltpu.VMEM((half_units + 8, lane), f32),
            pltpu.VMEM((width // lane, lane), f32),
            pltpu.SemaphoreType.DMA(()),
        ],
        in_place=(2,),
    )
    got = exchange(sent, both)
    sent = call(total_kernel, ((split, unit_pad, lane), bf16), [got, resid_units])
    got = exchange(sent, both)
    layer_out = call(
        gather_kernel,
        ((rows, width), bf16),
        [got],
        [pltpu.VMEM((narrow_size, half_units, lane), f32)],
    )
    return (attn_mixed, layer_out)


def solution(mesh):
    in_specs = (
        P("pool", None),
        P(),
        P("narrow", "wide", None, None),
        P(),
        P(),
        P("pool", "wide", "narrow", None),
        P("pool", "wide", "narrow", None),
        P(),
        P(),
        P("wide", None),
        P(),
        P(None, None, ("wide", "narrow")),
        P(("wide", "narrow"), None),
    )
    out_specs = (P("pool", None), P("pool", None))
    return jax.shard_map(
        per_device, mesh=mesh, in_specs=in_specs, out_specs=out_specs, check_vma=False
    )
```
